32 devices in a mesh: dp: 2 (over x), fsdp: 16 (over z, y, core).
Axes of the slice: x: 2, y: 2, z: 4, core: 2. Of those that a mesh axis runs over, the one named last changes fastest.
Arguments:
- rows: bfloat16 [32768, 1024], P(('dp', 'fsdp')), may hold values from -6 to 6
- segments: int32 [64, 512], P(('dp', 'fsdp')), may hold values from 0 to 3, never falling along the last dimension, each value on 1 to 256 neighbouring positions
- norm_gains: float32 [2, 1024], replicated, may hold values from 0.25 to 1.75
- w_query: bfloat16 [1024, 1024], P('dp', 'fsdp'), may hold values from -0.1875 to 0.1875
- w_key: bfloat16 [1024, 1024], P('dp', 'fsdp'), may hold values from -0.1875 to 0.1875
- w_value: bfloat16 [1024, 1024], P('dp', 'fsdp'), may hold values from -0.1875 to 0.1875
- w_output: bfloat16 [1024, 1024], P('dp', 'fsdp'), may hold values from -1.5 to 1.5
- w_gate: bfloat16 [1024, 4096], P('dp', 'fsdp'), may hold values from -0.1875 to 0.1875
- w_up: bfloat16 [1024, 4096], P('dp', 'fsdp'), may hold values from -0.1875 to 0.1875
- w_down: bfloat16 [4096, 1024], P('dp', 'fsdp'), may hold values from -0.125 to 0.125
- cotangent: bfloat16 [32768, 1024], P(('dp', 'fsdp')), may hold values from -6 to 6
Outputs:
- layer_out: bfloat16 [32768, 1024], P(('dp', 'fsdp'))
- rows_grad: float32 [32768, 1024], P(('dp', 'fsdp'))
- gains_grad: float32 [2, 1024], replicated
- query_grad: float32 [1024, 1024], P('dp', 'fsdp')
- key_grad: float32 [1024, 1024], P('dp', 'fsdp')
- value_grad: float32 [1024, 1024], P('dp', 'fsdp')
- output_grad: float32 [1024, 1024], P('dp', 'fsdp')
- gate_grad: float32 [1024, 4096], P('dp', 'fsdp')
- up_grad: float32 [1024, 4096], P('dp', 'fsdp')
- down_grad: float32 [4096, 1024], P('dp', 'fsdp')
The draws below stay inside these ranges and needn't reach their ends.
Inputs may be any that keep to these rules, and one draw needn't show every extreme that they name: `segments`: within each sequence the document numbers never fall, every number from 0 to 3 has 1 to 256 rows, and one document has exactly 256 rows.
All inputs are finite; a program needn't handle non-finite values.
Results may differ from the reference program's by a relative error of at most 0.012.
Values may be sent and summed in bfloat16 or wider, within the bound.
No kernel may reach another device: no remote copies, remote signals or barrier semaphores. Data moves between devices by JAX's collectives and lax.ppermute only.
A program may use at most 256 MiB of HBM per device.

```python
import math
import jax
import jax.numpy as jnp
import numpy as np
from jax import lax

D = 1024
HEADS = 16
HD = 64
FF = 4096
SEQ = 512
DOCS = 4
DOC_MOST = 256
NSEQ = 64
TOKENS = 32768


def strengthened(values, key, source, target, parts, factor):
    def block_of(axis_at):
        return (jnp.arange(values.shape[axis_at]) // (values.shape[axis_at] // parts)).reshape((-1,) + (1,) * (values.ndim - 1 - axis_at))

    first = jax.random.permutation(key, parts)[block_of(target)]
    other_side = (block_of(target) + parts // 2) % parts
    return jnp.where((block_of(source) == first) | (block_of(source) == other_side), factor * values, values)


def level_of(own_key, extent, shards, least, high):
    gain = 1.0
    for axis_at, shards_of in shards:
        draws = jax.random.uniform(jax.random.fold_in(jax.random.fold_in(own_key, 6), axis_at), (shards_of,), jnp.float32, least / len(shards), high / len(shards))
        gain = gain * jnp.repeat(jnp.exp(draws), extent[axis_at] // shards_of).reshape((-1,) + (1,) * (len(extent) - 1 - axis_at))
    return gain


def profile(amount, total, most, skew):
    weights = [(1 << 20) // math.isqrt(standing ** skew) + 1 for standing in range(2, amount + 1)]
    rest, given = total - most - (amount - 1), [1] * (amount - 1)
    while rest > 0:
        free = [i for i in range(amount - 1) if given[i] < most]
        whole, remaining = sum([weights[i] for i in free]), rest
        for i in free:
            more = min(most - given[i], max(1, remaining * weights[i] // whole), rest)
            given[i] = given[i] + more
            rest = rest - more
    return np.array([most] + given)


def uneven_parts(rng, count, total, bound, slope):
    if count == 2:
        one = jax.random.randint(rng, (), max(1, total - bound), min(bound, total - 1) + 1)
        return jnp.stack([one, total - one])
    tallies = jnp.asarray(profile(count, total, bound, slope), jnp.int32)
    couples = (count - 1) // 2
    giver, taker = tallies[1:1 + 2 * couples:2], tallies[2:2 + 2 * couples:2]
    margin = jnp.minimum(giver - 1, bound - taker)
    moved = jax.random.randint(jax.random.fold_in(rng, 1), (couples,), 0, 1 << 20) % (margin + 1)
    tallies = tallies.at[1:1 + 2 * couples:2].set(giver - moved).at[2:2 + 2 * couples:2].set(taker + moved)
    return tallies[jax.random.permutation(jax.random.fold_in(rng, 2), count)]


def centred(stream_key, shape, scale, reach, cuts=(), kind=jnp.bfloat16):
    level = level_of(stream_key, shape, cuts, -0.22, 0.18) if cuts else 1.0
    array = jax.random.normal(stream_key, shape, jnp.float32) * scale * level
    return jnp.minimum(jnp.maximum(array, -reach), reach).astype(kind)


def noise_with(key, shape, spread, reach, pieces, heavy, dtype=jnp.bfloat16):
    values = spread * jax.random.normal(key, shape, jnp.float32)
    if pieces:
        values = values * level_of(key, shape, pieces, -0.22, 0.18)
    return jnp.clip(strengthened(values, jax.random.fold_in(key, 3), *heavy), -reach, reach).astype(dtype)


def setup_inputs(seed: int = 0) -> dict:
    key_list = jax.random.split(jax.random.key(seed), 12)
    return {
        "rows": noise_with(key_list[0], (TOKENS, D), 1.0, 6.0, ((0, 32),), (0, 1, 32, 2.75)),
        "segments": jax.vmap(lambda own: jnp.searchsorted(jnp.cumsum(uneven_parts(own, DOCS, SEQ, DOC_MOST, 2)), jnp.arange(SEQ), side="right"))(jax.random.split(key_list[1], NSEQ)).reshape((NSEQ, SEQ)).astype(jnp.int32),
        "norm_gains": jnp.clip(1.0 + 0.15 * jax.random.normal(key_list[2], (2, D), jnp.float32), 0.25, 1.75),
        "w_query": centred(key_list[3], (D, D), D ** -0.5, 0.1875, ((0, 2), (1, 16))),
        "w_key": centred(key_list[4], (D, D), D ** -0.5, 0.1875, ((0, 2), (1, 16))),
        "w_value": centred(key_list[5], (D, D), D ** -0.5, 0.1875, ((0, 2), (1, 16))),
        "w_output": centred(key_list[6], (D, D), (max(1, D // 64)) ** -0.5, 1.5, ((0, 2), (1, 16))),
        "w_gate": centred(key_list[7], (D, FF), D ** -0.5, 0.1875, ((0, 2), (1, 16))),
        "w_up": centred(key_list[8], (D, FF), D ** -0.5, 0.1875, ((0, 2), (1, 16))),
        "w_down": centred(key_list[9], (FF, D), (FF // 2) ** -0.5, 0.125, ((0, 2), (1, 16))),
        "cotangent": centred(key_list[10], (TOKENS, D), 1.0, 6.0, ((0, 32),)),
    }


epsilon = 1e-05
neg_big = -1e+30

@jax.custom_vjp
def low(v):
    return lax.optimization_barrier(v.astype(jnp.bfloat16)).astype(jnp.float32)

@jax.custom_vjp
def low_back(v):
    return v

def low_keep(v):
    return (low(v), None)

def low_pass(kept, grad):
    return (grad,)

def back_keep(v):
    return (v, None)

def back_low(kept, grad):
    return (low(grad),)
low.defvjp(low_keep, low_pass)
low_back.defvjp(back_keep, back_low)

def product(operand, matrix):
    return jnp.dot(operand, matrix, precision=lax.Precision.HIGHEST)

def rms_scale(features, gain_row):
    return features * lax.rsqrt(lax.optimization_barrier(jnp.mean(features * features, axis=-1, keepdims=True)) + epsilon) * gain_row

def block_layer(source, segment, gain_pair, weights):
    w_query, w_key, w_value, w_output, w_gate, w_up, w_down = weights
    groups, seq_rows, width = source.shape
    score_scale = 1.0 / math.sqrt(HD)
    normed = low(rms_scale(source, gain_pair[0]))

    def split_heads(matrix):
        return low_back(low(product(normed, matrix))).reshape(groups, seq_rows, HEADS, HD)
    queries = split_heads(w_query)
    key_heads = split_heads(w_key)
    value_heads = split_heads(w_value)
    raw_scores = jnp.einsum('gqhd,gkhd->ghqk', queries, key_heads, precision=lax.Precision.HIGHEST)
    scores = low_back(raw_scores * score_scale)
    places = lax.broadcasted_iota(jnp.int32, (seq_rows, seq_rows), 0)
    columns = lax.broadcasted_iota(jnp.int32, (seq_rows, seq_rows), 1)
    allowed = (columns <= places)[None, None] & (segment[:, None, :, None] == segment[:, None, None, :])
    scores = jnp.where(allowed, scores, neg_big)
    attn_probs = low(jax.nn.softmax(scores, axis=-1))
    mixed_heads = jnp.einsum('ghqk,gkhd->gqhd', attn_probs, value_heads, precision=lax.Precision.HIGHEST)
    mixed_heads = low_back(low(mixed_heads.reshape(groups, seq_rows, width)))
    hidden = source + low_back(product(mixed_heads, w_output))
    normed_two = low(rms_scale(hidden, gain_pair[1]))
    gate_value = low_back(product(normed_two, w_gate))
    up_value = low_back(product(normed_two, w_up))
    inner_rows = low(jax.nn.silu(gate_value) * up_value)
    return hidden + low_back(product(inner_rows, w_down))

def reference(rows, segments, norm_gains, w_query, w_key, w_value, w_output, w_gate, w_up, w_down, cotangent):
    weights = (w_query.astype(jnp.float32), w_key.astype(jnp.float32), w_value.astype(jnp.float32), w_output.astype(jnp.float32), w_gate.astype(jnp.float32), w_up.astype(jnp.float32), w_down.astype(jnp.float32))
    gain_pair = norm_gains.astype(jnp.float32)
    total_seqs = segments.shape[0]
    seq_rows = segments.shape[1]
    width = rows.shape[1]
    group_size = math.gcd(total_seqs, max(1, 4096 // seq_rows))
    steps_count = total_seqs // group_size
    source = rows.astype(jnp.float32).reshape(steps_count, group_size, seq_rows, width)
    upstream = cotangent.astype(jnp.float32).reshape(steps_count, group_size, seq_rows, width)
    segment_groups = segments.reshape(steps_count, group_size, seq_rows)

    def scan_step(running, scan_item):
        source_part, segment, upstream_part = scan_item

        def forward(source_arg, gain_arg, weight_arg):
            return block_layer(source_arg, segment, gain_arg, weight_arg)
        result, pull_back = jax.vjp(forward, source_part, gain_pair, weights)
        grad_source, grad_gains, grad_weights = pull_back(upstream_part)
        running = (running[0] + grad_gains, tuple((total + extra for total, extra in zip(running[1], grad_weights))))
        return (running, (result, grad_source))
    starting = (jnp.zeros_like(gain_pair), tuple((jnp.zeros_like(matrix) for matrix in weights)))
    finished, stacked = lax.scan(scan_step, starting, (source, segment_groups, upstream))
    grad_gains, grad_weights = finished
    outputs, grad_rows = stacked
    return (outputs.reshape(-1, width).astype(jnp.bfloat16), grad_rows.reshape(-1, width), grad_gains, grad_weights[0], grad_weights[1], grad_weights[2], grad_weights[3], grad_weights[4], grad_weights[5], grad_weights[6])
```

```python
import math

import jax
import jax.numpy as jnp
from jax import lax
from jax.sharding import PartitionSpec as P

HEADS = 16
HD = 64


epsilon = 1e-05
neg_big = -1e30


def product_left(operand, matrix):
    return lax.dot_general(
        operand, matrix, (((0,), (0,)), ((), ())), preferred_element_type=jnp.float32
    )


def product(operand, matrix):
    return jnp.dot(operand, matrix, preferred_element_type=jnp.float32)


def product_right(operand, matrix):
    return lax.dot_general(
        operand, matrix, (((1,), (1,)), ((), ())), preferred_element_type=jnp.float32
    )


def norm_forward(features, gain_row):
    inverse = lax.rsqrt(jnp.mean(features * features, axis=-1, keepdims=True) + epsilon)
    return (features * inverse * gain_row, inverse)


def norm_backward(features, inverse, gain_row, upstream):
    scaled = features * inverse
    gain_term = jnp.sum(upstream * scaled, axis=0)
    inner_rows = upstream * gain_row
    back_rows = inverse * (
        inner_rows - scaled * jnp.mean(inner_rows * scaled, axis=-1, keepdims=True)
    )
    return (back_rows, gain_term)


def bits_of(count):
    amount = count.bit_length() - 1
    assert 1 << amount == count
    return amount


def swap(value, axis_name, mask):
    count = lax.axis_size(axis_name)
    return lax.ppermute(value, axis_name, [(i, i ^ mask) for i in range(count)])


def fetch_rows(shard):
    own = shard.T
    if lax.axis_size("dp") == 2:
        other = swap(own, "dp", 1)
        first = lax.axis_index("dp") == 0
        own = jnp.concatenate([jnp.where(first, own, other), jnp.where(first, other, own)], axis=1)
    else:
        own = lax.all_gather(own, "dp", axis=1, tiled=True)
    return lax.all_gather(own, "fsdp", axis=0, tiled=True)


def sum_terms(terms):
    total = terms[0].astype(jnp.float32)
    for term in terms[1:]:
        total = total + term.astype(jnp.float32)
    return total


def scatter_rows(partial, order):
    fsdp_bits = bits_of(lax.axis_size("fsdp"))
    dp_bits = bits_of(lax.axis_size("dp"))
    block = partial.shape[0] >> fsdp_bits
    width = partial.shape[1]
    place = {"fsdp": lax.axis_index("fsdp"), "dp": lax.axis_index("dp")}
    terms = [
        (
            partial.reshape((2,) * fsdp_bits + (block, width)),
            list(range(fsdp_bits - 1, -1, -1)),
            list(range(dp_bits - 1, -1, -1)),
        )
    ]
    left = {
        "fsdp": list(range(fsdp_bits - 1, -1, -1)),
        "dp": list(range(dp_bits - 1, -1, -1)),
    }

    def part_of(term, flipped):
        array, own_bits, own_dp = term
        starts, sizes = [], []
        for bit in own_bits:
            if bit in left["fsdp"] and ("fsdp", bit) != flipped:
                starts.append(0)
                sizes.append(2)
            else:
                value = (place["fsdp"] >> bit) & 1
                starts.append(1 - value if ("fsdp", bit) == flipped else value)
                sizes.append(1)
        span = array.shape[-1]
        offset = 0
        for bit in own_dp:
            if bit not in left["dp"] or ("dp", bit) == flipped:
                span //= 2
                value = (place["dp"] >> bit) & 1
                offset = offset + span * (1 - value if ("dp", bit) == flipped else value)
        starts += [0, offset]
        sizes += [block, span]
        taken = lax.dynamic_slice(array, starts, sizes)
        kept = [bit for bit in left["fsdp"] if ("fsdp", bit) != flipped]
        return taken.reshape((2,) * len(kept) + (block, span))

    for axis_name, bit in order:
        sent = sum_terms([part_of(term, (axis_name, bit)) for term in terms]).astype(jnp.bfloat16)
        received = swap(sent, axis_name, 1 << bit)
        left[axis_name].remove(bit)
        terms.append((received, list(left["fsdp"]), list(left["dp"])))
    return sum_terms([part_of(term, None) for term in terms]).T


def all_sum(value):
    for axis_name in ("fsdp", "dp"):
        for bit in range(bits_of(lax.axis_size(axis_name))):
            value = value + swap(value, axis_name, 1 << bit)
    return value


def exchange_orders():
    fsdp_bits = bits_of(lax.axis_size("fsdp"))
    dp_steps = [("dp", bit) for bit in range(bits_of(lax.axis_size("dp")) - 1, -1, -1)]
    first = [("fsdp", 0)]
    second = [("fsdp", 1)]
    rest = [("fsdp", bit) for bit in range(2, fsdp_bits)]
    return (first + second + dp_steps + rest, first + dp_steps + second + rest)


def masked_scores(queries, key_heads, segment, score_scale):
    seq_rows = segment.shape[1]
    scores = (
        jnp.einsum("gqhd,gkhd->ghqk", queries, key_heads, preferred_element_type=jnp.float32)
        * score_scale
    )
    places = lax.broadcasted_iota(jnp.int32, (seq_rows, seq_rows), 0)
    columns = lax.broadcasted_iota(jnp.int32, (seq_rows, seq_rows), 1)
    allowed = (columns <= places)[None] & (segment[:, :, None] == segment[:, None, :])
    return jnp.where(allowed[:, None], scores, neg_big)


def attention_forward(queries, key_heads, value_heads, segments, score_scale):
    groups, seq_rows = segments.shape
    split = (groups, seq_rows, HEADS, HD)
    queries, key_heads, value_heads = (
        array.reshape(split) for array in (queries, key_heads, value_heads)
    )
    scores = masked_scores(queries, key_heads, segments, score_scale)
    row_peak = jnp.max(scores, axis=-1, keepdims=True)
    log_total = row_peak + jnp.log(jnp.sum(jnp.exp(scores - row_peak), axis=-1, keepdims=True))
    attn_probs = jnp.exp(scores - log_total).astype(jnp.bfloat16)
    mixed = jnp.einsum(
        "ghqk,gkhd->gqhd", attn_probs, value_heads, preferred_element_type=jnp.float32
    )
    return mixed.reshape(groups * seq_rows, HEADS * HD).astype(jnp.bfloat16), log_total


def attention_backward(queries, key_heads, value_heads, log_total, segments, grad_mixed, score_scale):
    groups, seq_rows = segments.shape
    split = (groups, seq_rows, HEADS, HD)
    width = HEADS * HD
    queries, key_heads, value_heads, grad_mixed = (
        array.reshape(split) for array in (queries, key_heads, value_heads, grad_mixed)
    )
    probs = jnp.exp(masked_scores(queries, key_heads, segments, score_scale) - log_total)
    grad_values = jnp.einsum(
        "ghqk,gqhd->gkhd", probs.astype(jnp.bfloat16), grad_mixed, preferred_element_type=jnp.float32
    )
    grad_probs = jnp.einsum(
        "gqhd,gkhd->ghqk", grad_mixed, value_heads, preferred_element_type=jnp.float32
    )
    grad_scores = probs * (grad_probs - jnp.sum(probs * grad_probs, axis=-1, keepdims=True))
    grad_scores = grad_scores.astype(jnp.bfloat16)
    grad_queries = jnp.einsum(
        "ghqk,gkhd->gqhd", grad_scores, key_heads, preferred_element_type=jnp.float32
    )
    grad_keys = jnp.einsum(
        "ghqk,gqhd->gkhd", grad_scores, queries, preferred_element_type=jnp.float32
    )
    return (
        (grad_queries * score_scale).astype(jnp.bfloat16).reshape(-1, width),
        (grad_keys * score_scale).astype(jnp.bfloat16).reshape(-1, width),
        grad_values.astype(jnp.bfloat16).reshape(-1, width),
    )


def per_device(
    rows, segments, norm_gains, w_query, w_key, w_value, w_output, w_gate, w_up, w_down, cotangent
):
    score_scale = 1.0 / math.sqrt(HD)
    gain_attn = norm_gains[0]
    gain_mlp = norm_gains[1]
    order_a, order_b = exchange_orders()
    full_query = fetch_rows(w_query)
    full_key = fetch_rows(w_key)
    full_value = fetch_rows(w_value)
    full_output = fetch_rows(w_output)
    full_gate = fetch_rows(w_gate)
    full_up = fetch_rows(w_up)
    full_down = fetch_rows(w_down)

    source = rows.astype(jnp.float32)
    normed, inverse_attn = norm_forward(source, gain_attn)
    normed_b = normed.astype(jnp.bfloat16)
    queries = product_right(normed_b, full_query).astype(jnp.bfloat16)
    key_heads = product_right(normed_b, full_key).astype(jnp.bfloat16)
    value_heads = product_right(normed_b, full_value).astype(jnp.bfloat16)
    mixed_heads, log_total = attention_forward(
        queries, key_heads, value_heads, segments, score_scale
    )
    hidden = source + product_right(mixed_heads, full_output)
    normed_two, inverse_mlp = norm_forward(hidden, gain_mlp)
    normed_two_b = normed_two.astype(jnp.bfloat16)
    gate_value = product_right(normed_two_b, full_gate)
    up_value = product_right(normed_two_b, full_up)
    sigmoid_gate = jax.nn.sigmoid(gate_value)
    activated = gate_value * sigmoid_gate
    inner_rows = (activated * up_value).astype(jnp.bfloat16)
    result = hidden + product_right(inner_rows, full_down)
    layer_out = result.astype(jnp.bfloat16)

    grad_out = cotangent.astype(jnp.float32)
    down_grad = scatter_rows(
        product_left(cotangent, inner_rows).astype(jnp.bfloat16), order_a
    )
    grad_inner = product(cotangent, full_down)
    grad_up = (grad_inner * activated).astype(jnp.bfloat16)
    grad_gate = (
        grad_inner * up_value * sigmoid_gate * (1.0 + gate_value * (1.0 - sigmoid_gate))
    ).astype(jnp.bfloat16)
    gate_grad = scatter_rows(
        product_left(grad_gate, normed_two_b).astype(jnp.bfloat16), order_b
    )
    up_grad = scatter_rows(product_left(grad_up, normed_two_b).astype(jnp.bfloat16), order_a)
    grad_normed_two = product(grad_gate, full_gate) + product(grad_up, full_up)
    back_mlp, gain_mlp_term = norm_backward(hidden, inverse_mlp, gain_mlp, grad_normed_two)
    grad_hidden = grad_out + back_mlp
    grad_hidden_b = grad_hidden.astype(jnp.bfloat16)
    output_grad = scatter_rows(
        product_left(grad_hidden_b, mixed_heads).astype(jnp.bfloat16), order_b
    )
    grad_mixed = product(grad_hidden_b, full_output).astype(jnp.bfloat16)
    grad_queries, grad_keys, grad_values = attention_backward(
        queries, key_heads, value_heads, log_total, segments, grad_mixed, score_scale
    )
    query_grad = scatter_rows(product_left(grad_queries, normed_b).astype(jnp.bfloat16), order_a)
    key_grad = scatter_rows(product_left(grad_keys, normed_b).astype(jnp.bfloat16), order_b)
    value_grad = scatter_rows(product_left(grad_values, normed_b).astype(jnp.bfloat16), order_a)
    grad_normed = (
        product(grad_queries, full_query)
        + product(grad_keys, full_key)
        + product(grad_values, full_value)
    )
    back_attn, gain_attn_term = norm_backward(source, inverse_attn, gain_attn, grad_normed)
    rows_grad = grad_hidden + back_attn
    gains_grad = all_sum(jnp.stack([gain_attn_term, gain_mlp_term]))
    return (
        layer_out,
        rows_grad,
        gains_grad,
        query_grad,
        key_grad,
        value_grad,
        output_grad,
        gate_grad,
        up_grad,
        down_grad,
    )


def solution(mesh):
    split_rows = P(("dp", "fsdp"), None)
    split_weight = P("dp", "fsdp")
    return jax.shard_map(
        per_device,
        mesh=mesh,
        in_specs=(split_rows, split_rows, P()) + (split_weight,) * 7 + (split_rows,),
        out_specs=(split_rows, split_rows, P()) + (split_weight,) * 7,
        check_vma=False,
    )
```

```python
import functools
import math

import jax
import jax.numpy as jnp
from jax import lax
from jax.experimental import pallas as pl
from jax.experimental.pallas import tpu as pltpu
from jax.sharding import PartitionSpec as P

HEADS = 16
HD = 64


epsilon = 1e-05
neg_big = -1e30


def product_left(operand, matrix):
    return lax.dot_general(
        operand, matrix, (((0,), (0,)), ((), ())), preferred_element_type=jnp.float32
    )


def product(operand, matrix):
    return jnp.dot(operand, matrix, preferred_element_type=jnp.float32)


def product_right(operand, matrix):
    return lax.dot_general(
        operand, matrix, (((1,), (1,)), ((), ())), preferred_element_type=jnp.float32
    )


def norm_forward(features, gain_row):
    inverse = lax.rsqrt(jnp.mean(features * features, axis=-1, keepdims=True) + epsilon)
    return (features * inverse * gain_row, inverse)


def norm_backward(features, inverse, gain_row, upstream):
    scaled = features * inverse
    gain_term = jnp.sum(upstream * scaled, axis=0)
    inner_rows = upstream * gain_row
    back_rows = inverse * (
        inner_rows - scaled * jnp.mean(inner_rows * scaled, axis=-1, keepdims=True)
    )
    return (back_rows, gain_term)


def bits_of(count):
    amount = count.bit_length() - 1
    assert 1 << amount == count
    return amount


def swap(value, axis_name, mask):
    count = lax.axis_size(axis_name)
    return lax.ppermute(value, axis_name, [(i, i ^ mask) for i in range(count)])


def fetch_rows(shard):
    own = shard.T
    if lax.axis_size("dp") == 2:
        other = swap(own, "dp", 1)
        first = lax.axis_index("dp") == 0
        own = jnp.concatenate([jnp.where(first, own, other), jnp.where(first, other, own)], axis=1)
    else:
        own = lax.all_gather(own, "dp", axis=1, tiled=True)
    return lax.all_gather(own, "fsdp", axis=0, tiled=True)


def sum_terms(terms):
    total = terms[0].astype(jnp.float32)
    for term in terms[1:]:
        total = total + term.astype(jnp.float32)
    return total


def scatter_rows(partial, order):
    fsdp_bits = bits_of(lax.axis_size("fsdp"))
    dp_bits = bits_of(lax.axis_size("dp"))
    block = partial.shape[0] >> fsdp_bits
    width = partial.shape[1]
    place = {"fsdp": lax.axis_index("fsdp"), "dp": lax.axis_index("dp")}
    terms = [
        (
            partial.reshape((2,) * fsdp_bits + (block, width)),
            list(range(fsdp_bits - 1, -1, -1)),
            list(range(dp_bits - 1, -1, -1)),
        )
    ]
    left = {
        "fsdp": list(range(fsdp_bits - 1, -1, -1)),
        "dp": list(range(dp_bits - 1, -1, -1)),
    }

    def part_of(term, flipped):
        array, own_bits, own_dp = term
        starts, sizes = [], []
        for bit in own_bits:
            if bit in left["fsdp"] and ("fsdp", bit) != flipped:
                starts.append(0)
                sizes.append(2)
            else:
                value = (place["fsdp"] >> bit) & 1
                starts.append(1 - value if ("fsdp", bit) == flipped else value)
                sizes.append(1)
        span = array.shape[-1]
        offset = 0
        for bit in own_dp:
            if bit not in left["dp"] or ("dp", bit) == flipped:
                span //= 2
                value = (place["dp"] >> bit) & 1
                offset = offset + span * (1 - value if ("dp", bit) == flipped else value)
        starts += [0, offset]
        sizes += [block, span]
        taken = lax.dynamic_slice(array, starts, sizes)
        kept = [bit for bit in left["fsdp"] if ("fsdp", bit) != flipped]
        return taken.reshape((2,) * len(kept) + (block, span))

    for axis_name, bit in order:
        sent = sum_terms([part_of(term, (axis_name, bit)) for term in terms]).astype(jnp.bfloat16)
        received = swap(sent, axis_name, 1 << bit)
        left[axis_name].remove(bit)
        terms.append((received, list(left["fsdp"]), list(left["dp"])))
    return sum_terms([part_of(term, None) for term in terms]).T


def all_sum(value):
    for axis_name in ("fsdp", "dp"):
        for bit in range(bits_of(lax.axis_size(axis_name))):
            value = value + swap(value, axis_name, 1 << bit)
    return value


def exchange_orders():
    fsdp_bits = bits_of(lax.axis_size("fsdp"))
    dp_steps = [("dp", bit) for bit in range(bits_of(lax.axis_size("dp")) - 1, -1, -1)]
    first = [("fsdp", 0)]
    second = [("fsdp", 1)]
    rest = [("fsdp", bit) for bit in range(2, fsdp_bits)]
    return (first + second + dp_steps + rest, first + dp_steps + second + rest)


def masked_scores(queries, key_heads, segment, score_scale):
    seq_rows = segment.shape[1]
    scores = (
        jnp.einsum("gqhd,gkhd->ghqk", queries, key_heads, preferred_element_type=jnp.float32)
        * score_scale
    )
    places = lax.broadcasted_iota(jnp.int32, (seq_rows, seq_rows), 0)
    columns = lax.broadcasted_iota(jnp.int32, (seq_rows, seq_rows), 1)
    allowed = (columns <= places)[None] & (segment[:, :, None] == segment[:, None, :])
    return jnp.where(allowed[:, None], scores, neg_big)


def dot_of(left, right, left_dim, right_dim):
    return lax.dot_general(
        left, right, (((left_dim,), (right_dim,)), ((), ())), preferred_element_type=jnp.float32
    )


def allowed_block(rows_first, columns_first, row_segments, column_segments):
    shape = (row_segments.shape[0], column_segments.shape[1])
    places = rows_first + lax.broadcasted_iota(jnp.int32, shape, 0)
    columns = columns_first + lax.broadcasted_iota(jnp.int32, shape, 1)
    return (columns <= places) & (row_segments == column_segments)


def attention_forward_kernel(row_seg_ref, col_seg_ref, q_ref, k_ref, v_ref, o_ref, log_ref, *, block):
    seq_rows = q_ref.shape[0]
    heads_here = q_ref.shape[1] // HD
    score_scale = 1.0 / math.sqrt(HD)
    for first in range(0, seq_rows, block):
        last = first + block
        allowed = allowed_block(first, 0, row_seg_ref[first:last, :], col_seg_ref[0, :, :last])
        outs, logs = [], []
        for head in range(heads_here):
            lanes = slice(head * HD, (head + 1) * HD)
            scores = dot_of(q_ref[first:last, lanes], k_ref[:last, lanes], 1, 1) * score_scale
            scores = jnp.where(allowed, scores, neg_big)
            peak = jnp.max(scores, axis=-1, keepdims=True)
            powers = jnp.exp(scores - peak)
            total = jnp.sum(powers, axis=-1, keepdims=True)
            probs = (powers * (1.0 / total)).astype(jnp.bfloat16)
            outs.append(dot_of(probs, v_ref[:last, lanes], 1, 0))
            logs.append(peak + jnp.log(total))
        o_ref[first:last, :] = jnp.concatenate(outs, axis=1).astype(jnp.bfloat16)
        log_ref[0, first:last, :] = jnp.concatenate(logs, axis=1)


def attention_backward_kernel(
    row_seg_ref, col_seg_ref, q_ref, k_ref, v_ref, g_ref, log_ref, out_ref, *, block
):
    seq_rows = q_ref.shape[0]
    heads_here = q_ref.shape[1] // HD
    score_scale = 1.0 / math.sqrt(HD)
    dk_sums = [[None] * (seq_rows // block) for _ in range(heads_here)]
    dv_sums = [[None] * (seq_rows // block) for _ in range(heads_here)]
    for first in range(0, seq_rows, block):
        last = first + block
        allowed = allowed_block(first, 0, row_seg_ref[first:last, :], col_seg_ref[0, :, :last])
        dqs = []
        for head in range(heads_here):
            lanes = slice(head * HD, (head + 1) * HD)
            queries = q_ref[first:last, lanes]
            key_part = k_ref[:last, lanes]
            upstream = g_ref[first:last, lanes]
            scores = dot_of(queries, key_part, 1, 1) * score_scale
            scores = jnp.where(allowed, scores, neg_big)
            probs = jnp.exp(scores - log_ref[0, first:last, head : head + 1])
            grad_probs = dot_of(upstream, v_ref[:last, lanes], 1, 1)
            inner = jnp.sum(probs * grad_probs, axis=-1, keepdims=True)
            grad_scores = (probs * (grad_probs - inner)).astype(jnp.bfloat16)
            probs_b = probs.astype(jnp.bfloat16)
            dqs.append(dot_of(grad_scores, key_part, 1, 0) * score_scale)
            dv_part = dot_of(probs_b, upstream, 0, 0)
            dk_part = dot_of(grad_scores, queries, 0, 0)
            for index in range(last // block):
                span = slice(index * block, (index + 1) * block)
                old_v, old_k = dv_sums[head][index], dk_sums[head][index]
                dv_sums[head][index] = dv_part[span] if old_v is None else old_v + dv_part[span]
                dk_sums[head][index] = dk_part[span] if old_k is None else old_k + dk_part[span]
        out_ref[0, first:last, :] = jnp.concatenate(dqs, axis=1).astype(jnp.bfloat16)
    for index in range(seq_rows // block):
        span = slice(index * block, (index + 1) * block)
        out_ref[1, span, :] = (
            jnp.concatenate([dk_sums[head][index] for head in range(heads_here)], axis=1)
            * score_scale
        ).astype(jnp.bfloat16)
        out_ref[2, span, :] = jnp.concatenate(
            [dv_sums[head][index] for head in range(heads_here)], axis=1
        ).astype(jnp.bfloat16)


PAIR = 2


def attention_call(kernel, operands, segments, outputs, log_operand):
    groups, seq_rows = segments.shape
    lanes = PAIR * HD
    seq_block = pl.BlockSpec((seq_rows, lanes), lambda group, pair: (group, pair))
    log_block = pl.BlockSpec((1, seq_rows, PAIR), lambda group, pair: (pair, group, 0))
    row_block = pl.BlockSpec((seq_rows, 1), lambda group, pair: (group, 0))
    col_block = pl.BlockSpec((1, 1, seq_rows), lambda group, pair: (group, 0, 0))
    rows = groups * seq_rows
    wide = jax.ShapeDtypeStruct((rows, HEADS * HD), jnp.bfloat16)
    three_block = pl.BlockSpec((3, seq_rows, lanes), lambda group, pair: (0, group, pair))
    specs = {
        "seq": (seq_block, wide),
        "log": (log_block, jax.ShapeDtypeStruct((HEADS // PAIR, rows, PAIR), jnp.float32)),
        "three": (three_block, jax.ShapeDtypeStruct((3, rows, HEADS * HD), jnp.bfloat16)),
    }
    return pl.pallas_call(
        functools.partial(kernel, block=min(256, seq_rows)),
        grid=(groups, HEADS // PAIR),
        in_specs=[row_block, col_block]
        + [seq_block] * len(operands)
        + [log_block] * (log_operand is not None),
        out_specs=[specs[kind][0] for kind in outputs],
        out_shape=[specs[kind][1] for kind in outputs],
        name=kernel.__name__,
    )(
        segments.reshape(rows, 1),
        segments.reshape(groups, 1, seq_rows),
        *operands,
        *(() if log_operand is None else (log_operand,)),
    )


def attention_forward(queries, key_heads, value_heads, segments, score_scale):
    return attention_call(
        attention_forward_kernel, (queries, key_heads, value_heads), segments, ("seq", "log"), None
    )


def attention_backward(queries, key_heads, value_heads, log_total, segments, grad_mixed, score_scale):
    return attention_call(
        attention_backward_kernel,
        (queries, key_heads, value_heads, grad_mixed),
        segments,
        ("three",),
        log_total,
    )[0]


def fetch_pairs(shards, places, y_first):
    own = jnp.concatenate([shard.T for shard in shards], axis=0)[None]
    heights = [shard.shape[1] for shard in shards]
    for mask in (8, 4):
        own = jnp.concatenate([own, swap(own, "fsdp", mask)], axis=0)
    steps = [("dp", 1), ("fsdp", 2)]
    if y_first:
        steps = steps[::-1]
    own = jnp.stack([own, swap(own, *steps[0])])
    pieces = [own, swap(own, *steps[1])]
    pieces += [swap(piece, "fsdp", 1) for piece in pieces]
    return assemble(pieces, heights, places, y_first)


def assemble_kernel(place_ref, *refs, heights, y_first):
    piece_refs, out_refs = refs[:4], refs[4:]
    half = piece_refs[0].shape[-1]
    own_y, own_core, own_x = place_ref[4], place_ref[5], place_ref[6]
    for index, piece_ref in enumerate(piece_refs):
        second, core = index % 2, own_core ^ (index // 2)
        for first in range(2):
            y, x = (first, second) if y_first else (second, first)
            lanes = pl.ds(pl.multiple_of((own_x ^ x) * half, half), half)
            start = 0
            for height, out_ref in zip(heights, out_refs):
                out_ref[0, own_y ^ y, core, :, lanes] = piece_ref[first, 0, start : start + height, :]
                start += height


def assemble(pieces, heights, places, y_first):
    _, zs, height, half = pieces[0].shape
    outs = pl.pallas_call(
        functools.partial(assemble_kernel, heights=heights, y_first=y_first),
        grid_spec=pltpu.PrefetchScalarGridSpec(
            num_scalar_prefetch=1,
            grid=(zs,),
            in_specs=[pl.BlockSpec((2, 1, height, half), lambda i, place: (0, i, 0, 0))] * 4,
            out_specs=[
                pl.BlockSpec((1, 2, 2, part, 2 * half), lambda i, place: (place[i], 0, 0, 0, 0))
                for part in heights
            ],
        ),
        out_shape=[
            jax.ShapeDtypeStruct((zs, 2, 2, part, 2 * half), jnp.bfloat16) for part in heights
        ],
        name="assemble",
    )(places, *pieces)
    return [out.reshape(-1, 2 * half) for out in outs]


def relative_places():
    at = lax.axis_index("fsdp")
    z, y, core = at >> 2, (at >> 1) & 1, at & 1
    zs = [z ^ (j >> 1) ^ ((j & 1) << 1) for j in range(4)]
    return jnp.stack([*zs, y, core, lax.axis_index("dp")]).astype(jnp.int32)


def grad_kernel(table_ref, kept_table_ref, d_ref, act_ref, out_ref):
    out_ref[0] = dot_of(d_ref[...], act_ref[...], 0, 0).astype(jnp.bfloat16)


def grad_blocks(upstream, acts, blocks, act_blocks):
    rows, width = acts.shape
    height = upstream.shape[1] // lax.axis_size("fsdp")
    part = width // act_blocks.shape[0]
    count = blocks.shape[0]
    return pl.pallas_call(
        grad_kernel,
        grid_spec=pltpu.PrefetchScalarGridSpec(
            num_scalar_prefetch=2,
            grid=(act_blocks.shape[0], count),
            in_specs=[
                pl.BlockSpec((rows, height), lambda k, i, table, acts_at: (0, table[i])),
                pl.BlockSpec((rows, part), lambda k, i, table, acts_at: (0, acts_at[k])),
            ],
            out_specs=pl.BlockSpec((1, height, part), lambda k, i, table, acts_at: (i, 0, k)),
        ),
        out_shape=jax.ShapeDtypeStruct((count, height, width), jnp.bfloat16),
        name="weight_grad",
    )(blocks, act_blocks, upstream, acts)


def grad_pair_kernel(table_ref, acts_at_ref, core_ref, d0_ref, d1_ref, act_ref, sent_ref, kept_ref, sums_ref):
    pair = jnp.concatenate([d0_ref[0], d1_ref[0]], axis=1)
    sums_ref[...] = dot_of(pair, act_ref[...], 0, 0)
    height = kept_ref.shape[-2]
    core = core_ref[0]
    for index in range(2):
        base = index * 2 * height
        kept_at = pl.multiple_of(base + core * height, height)
        sent_at = pl.multiple_of(base + (1 - core) * height, height)
        kept_ref[index, 0] = sums_ref[pl.ds(kept_at, height), :].astype(jnp.bfloat16)
        sent_ref[index, 0] = sums_ref[pl.ds(sent_at, height), :].astype(jnp.bfloat16)


def grad_pairs(upstream, acts, pairs, act_blocks, core):
    rows, width = acts.shape
    many = upstream.shape[0]
    height = upstream.shape[2] // lax.axis_size("fsdp")
    part = width // act_blocks.shape[0]
    count = pairs.shape[0]
    shape = jax.ShapeDtypeStruct((count, many, height, width), jnp.bfloat16)
    out_block = pl.BlockSpec((2, 1, height, part), lambda k, m, i, *tables: (i, m, 0, k))
    return pl.pallas_call(
        grad_pair_kernel,
        grid_spec=pltpu.PrefetchScalarGridSpec(
            num_scalar_prefetch=3,
            grid=(act_blocks.shape[0], many, count // 2),
            in_specs=[
                pl.BlockSpec((1, rows, 2 * height), lambda k, m, i, table, *_: (m, 0, table[2 * i])),
                pl.BlockSpec(
                    (1, rows, 2 * height), lambda k, m, i, table, *_: (m, 0, table[2 * i + 1])
                ),
                pl.BlockSpec((rows, part), lambda k, m, i, table, acts_at, _: (0, acts_at[k])),
            ],
            out_specs=[out_block, out_block],
            scratch_shapes=[pltpu.VMEM((4 * height, part), jnp.float32)],
        ),
        out_shape=[shape, shape],
        name="weight_grad_pairs",
    )(pairs, act_blocks, core, upstream, upstream, acts)


def scatter_pairs(sent, kept, y_first):
    half = kept.shape[-1] // 2
    terms = [kept, swap(sent, "fsdp", 1)]
    yield sent
    for axis_name in ("fsdp", "dp") if y_first else ("dp", "fsdp"):
        if axis_name == "fsdp":
            given = sum_terms([term[4:] for term in terms]).astype(jnp.bfloat16)
            terms = [term[:4] for term in terms] + [swap(given, "fsdp", 2)]
        else:
            given = sum_terms([term[..., half:] for term in terms]).astype(jnp.bfloat16)
            terms = [term[..., :half] for term in terms] + [swap(given, "dp", 1)]
        yield given
    for mask, at in ((4, 2), (8, 1)):
        given = sum_terms([term[at : 2 * at] for term in terms]).astype(jnp.bfloat16)
        terms = [term[:at] for term in terms] + [swap(given, "fsdp", mask)]
        yield given
    yield sum_terms([term[0] for term in terms])


def grad_tables(places):
    z, y, core, x = places[:4], places[4], places[5], places[6:7]
    pairs = jnp.concatenate([z * 2 + y, z * 2 + (1 - y)])
    halves = jnp.concatenate([x, 1 - x])
    quarters = jnp.concatenate([2 * x, 2 * x + 1, 2 - 2 * x, 3 - 2 * x])
    return pairs, pairs * 2 + (1 - core), pairs * 2 + core, halves, quarters, places[5:6]


def tie(value, *earlier):
    return lax.optimization_barrier((value, *earlier))[0]


def per_device_paired(
    rows, segments, norm_gains, w_query, w_key, w_value, w_output, w_gate, w_up, w_down, cotangent
):
    score_scale = 1.0 / math.sqrt(HD)
    gain_attn = norm_gains[0]
    gain_mlp = norm_gains[1]
    places = relative_places()
    pairs, sent_blocks, kept_blocks, halves, quarters, core = grad_tables(places)
    full_query, full_key = fetch_pairs((w_query, w_key), places, False)
    full_value, full_output = fetch_pairs((w_value, w_output), places, True)
    (full_gate,) = fetch_pairs((w_gate,), places, False)
    (full_up,) = fetch_pairs((w_up,), places, True)
    (full_down,) = fetch_pairs((w_down,), places, False)

    source = rows.astype(jnp.float32)
    normed, inverse_attn = norm_forward(source, gain_attn)
    normed_b = normed.astype(jnp.bfloat16)
    queries = product_right(normed_b, full_query).astype(jnp.bfloat16)
    key_heads = product_right(normed_b, full_key).astype(jnp.bfloat16)
    value_heads = product_right(normed_b, full_value).astype(jnp.bfloat16)
    mixed_heads, log_total = attention_forward(
        queries, key_heads, value_heads, segments, score_scale
    )
    hidden = source + product_right(mixed_heads, full_output)
    normed_two, inverse_mlp = norm_forward(hidden, gain_mlp)
    normed_two_b = normed_two.astype(jnp.bfloat16)
    gate_value = product_right(normed_two_b, full_gate)
    up_value = product_right(normed_two_b, full_up)
    sigmoid_gate = jax.nn.sigmoid(gate_value)
    activated = gate_value * sigmoid_gate
    inner_rows = (activated * up_value).astype(jnp.bfloat16)

    grad_out = cotangent.astype(jnp.float32)
    down = scatter_pairs(*grad_pairs(cotangent[None], inner_rows, pairs, quarters, core), True)
    result = hidden + product_right(tie(inner_rows, next(down)), full_down)
    layer_out = result.astype(jnp.bfloat16)
    grad_inner = product(tie(cotangent, layer_out), full_down)
    grad_up = (grad_inner * activated).astype(jnp.bfloat16)
    grad_gate = (
        grad_inner * up_value * sigmoid_gate * (1.0 + gate_value * (1.0 - sigmoid_gate))
    ).astype(jnp.bfloat16)
    grad_gate = tie(grad_gate, next(down))
    gate_sent = grad_blocks(grad_gate, normed_two_b, sent_blocks, halves)
    gate_kept = grad_blocks(tie(grad_gate, gate_sent), normed_two_b, kept_blocks, halves)
    gate = scatter_pairs(gate_sent, gate_kept, False)
    next(gate)
    grad_up = tie(grad_up, gate_kept)
    up_sent = grad_blocks(grad_up, normed_two_b, sent_blocks, halves)
    grad_up_kept = tie(grad_up, up_sent, next(gate))
    up_kept = grad_blocks(grad_up_kept, normed_two_b, kept_blocks, halves)
    up = scatter_pairs(up_sent, up_kept, True)
    next(up)
    part = product(tie(grad_gate, up_kept), full_gate)
    grad_up = tie(grad_up, part, next(up))
    grad_normed_two = part + product(grad_up, full_up)
    grad_normed_two = tie(grad_normed_two, next(down))
    back_mlp, gain_mlp_term = norm_backward(hidden, inverse_mlp, gain_mlp, grad_normed_two)
    grad_hidden = grad_out + back_mlp
    grad_hidden_b = grad_hidden.astype(jnp.bfloat16)
    output = scatter_pairs(
        *grad_pairs(grad_hidden_b[None], mixed_heads, pairs, halves, core), False
    )
    grad_mixed = product(tie(grad_hidden_b, next(output)), full_output).astype(jnp.bfloat16)
    grad_mixed = tie(grad_mixed, next(gate), next(down), next(output))
    grad_attn = attention_backward(
        queries, key_heads, value_heads, log_total, segments, grad_mixed, score_scale
    )
    grad_attn = tie(grad_attn, next(up), next(gate), next(down), next(output))
    attn = scatter_pairs(*grad_pairs(grad_attn, normed_b, pairs, halves, core), True)
    grad_attn = tie(grad_attn, next(attn), next(up), next(gate), next(output))
    grad_normed = product(grad_attn[0], full_query) + product(grad_attn[1], full_key)
    grad_normed = grad_normed + product(tie(grad_attn, grad_normed, next(attn))[2], full_value)
    grad_normed = tie(grad_normed, next(up), next(output))
    back_attn, gain_attn_term = norm_backward(source, inverse_attn, gain_attn, grad_normed)
    rows_grad = grad_hidden + back_attn
    next(attn)
    gains_grad = all_sum(jnp.stack([gain_attn_term, gain_mlp_term]))
    up_sum, gate_sum, output_sum, down_sum = (list(one)[-1] for one in (up, gate, output, down))
    attn_sum = list(attn)[-1]
    return (
        layer_out,
        rows_grad,
        gains_grad,
        attn_sum[0].T,
        attn_sum[1].T,
        attn_sum[2].T,
        output_sum[0].T,
        gate_sum.T,
        up_sum.T,
        down_sum[0].T,
    )


def per_device_any(
    rows, segments, norm_gains, w_query, w_key, w_value, w_output, w_gate, w_up, w_down, cotangent
):
    score_scale = 1.0 / math.sqrt(HD)
    gain_attn = norm_gains[0]
    gain_mlp = norm_gains[1]
    order_a, order_b = exchange_orders()
    full_query = fetch_rows(w_query)
    full_key = fetch_rows(w_key)
    full_value = fetch_rows(w_value)
    full_output = fetch_rows(w_output)
    full_gate = fetch_rows(w_gate)
    full_up = fetch_rows(w_up)
    full_down = fetch_rows(w_down)

    source = rows.astype(jnp.float32)
    normed, inverse_attn = norm_forward(source, gain_attn)
    normed_b = normed.astype(jnp.bfloat16)
    queries = product_right(normed_b, full_query).astype(jnp.bfloat16)
    key_heads = product_right(normed_b, full_key).astype(jnp.bfloat16)
    value_heads = product_right(normed_b, full_value).astype(jnp.bfloat16)
    mixed_heads, log_total = attention_forward(
        queries, key_heads, value_heads, segments, score_scale
    )
    hidden = source + product_right(mixed_heads, full_output)
    normed_two, inverse_mlp = norm_forward(hidden, gain_mlp)
    normed_two_b = normed_two.astype(jnp.bfloat16)
    gate_value = product_right(normed_two_b, full_gate)
    up_value = product_right(normed_two_b, full_up)
    sigmoid_gate = jax.nn.sigmoid(gate_value)
    activated = gate_value * sigmoid_gate
    inner_rows = (activated * up_value).astype(jnp.bfloat16)
    result = hidden + product_right(inner_rows, full_down)
    layer_out = result.astype(jnp.bfloat16)

    grad_out = cotangent.astype(jnp.float32)
    down_grad = scatter_rows(
        product_left(cotangent, inner_rows).astype(jnp.bfloat16), order_a
    )
    grad_inner = product(cotangent, full_down)
    grad_up = (grad_inner * activated).astype(jnp.bfloat16)
    grad_gate = (
        grad_inner * up_value * sigmoid_gate * (1.0 + gate_value * (1.0 - sigmoid_gate))
    ).astype(jnp.bfloat16)
    gate_grad = scatter_rows(
        product_left(grad_gate, normed_two_b).astype(jnp.bfloat16), order_b
    )
    up_grad = scatter_rows(product_left(grad_up, normed_two_b).astype(jnp.bfloat16), order_a)
    grad_normed_two = product(grad_gate, full_gate) + product(grad_up, full_up)
    back_mlp, gain_mlp_term = norm_backward(hidden, inverse_mlp, gain_mlp, grad_normed_two)
    grad_hidden = grad_out + back_mlp
    grad_hidden_b = grad_hidden.astype(jnp.bfloat16)
    output_grad = scatter_rows(
        product_left(grad_hidden_b, mixed_heads).astype(jnp.bfloat16), order_b
    )
    grad_mixed = product(grad_hidden_b, full_output).astype(jnp.bfloat16)
    grad_queries, grad_keys, grad_values = attention_backward(
        queries, key_heads, value_heads, log_total, segments, grad_mixed, score_scale
    )
    query_grad = scatter_rows(product_left(grad_queries, normed_b).astype(jnp.bfloat16), order_a)
    key_grad = scatter_rows(product_left(grad_keys, normed_b).astype(jnp.bfloat16), order_b)
    value_grad = scatter_rows(product_left(grad_values, normed_b).astype(jnp.bfloat16), order_a)
    grad_normed = (
        product(grad_queries, full_query)
        + product(grad_keys, full_key)
        + product(grad_values, full_value)
    )
    back_attn, gain_attn_term = norm_backward(source, inverse_attn, gain_attn, grad_normed)
    rows_grad = grad_hidden + back_attn
    gains_grad = all_sum(jnp.stack([gain_attn_term, gain_mlp_term]))
    return (
        layer_out,
        rows_grad,
        gains_grad,
        query_grad,
        key_grad,
        value_grad,
        output_grad,
        gate_grad,
        up_grad,
        down_grad,
    )


def solution(mesh):
    split_rows = P(("dp", "fsdp"), None)
    split_weight = P("dp", "fsdp")
    paired = mesh.shape["dp"] == 2 and mesh.shape["fsdp"] == 16
    return jax.shard_map(
        per_device_paired if paired else per_device_any,
        mesh=mesh,
        in_specs=(split_rows, split_rows, P()) + (split_weight,) * 7 + (split_rows,),
        out_specs=(split_rows, split_rows, P()) + (split_weight,) * 7,
        check_vma=False,
    )
```

```python
import functools
import math

import jax
import jax.numpy as jnp
from jax import lax
from jax.experimental import pallas as pl
from jax.experimental.pallas import tpu as pltpu
from jax.sharding import PartitionSpec as P

HEADS = 16
HD = 64


epsilon = 1e-05
neg_big = -1e30


def product_left(operand, matrix):
    return lax.dot_general(
        operand, matrix, (((0,), (0,)), ((), ())), preferred_element_type=jnp.float32
    )


def product(operand, matrix):
    return jnp.dot(operand, matrix, preferred_element_type=jnp.float32)


def product_right(operand, matrix):
    return lax.dot_general(
        operand, matrix, (((1,), (1,)), ((), ())), preferred_element_type=jnp.float32
    )


def norm_forward(features, gain_row):
    inverse = lax.rsqrt(jnp.mean(features * features, axis=-1, keepdims=True) + epsilon)
    return (features * inverse * gain_row, inverse)


def norm_backward(features, inverse, gain_row, upstream):
    scaled = features * inverse
    gain_term = jnp.sum(upstream * scaled, axis=0)
    inner_rows = upstream * gain_row
    back_rows = inverse * (
        inner_rows - scaled * jnp.mean(inner_rows * scaled, axis=-1, keepdims=True)
    )
    return (back_rows, gain_term)


def bits_of(count):
    amount = count.bit_length() - 1
    assert 1 << amount == count
    return amount


def swap(value, axis_name, mask):
    count = lax.axis_size(axis_name)
    return lax.ppermute(value, axis_name, [(i, i ^ mask) for i in range(count)])


def fetch_rows(shard):
    own = shard.T
    if lax.axis_size("dp") == 2:
        other = swap(own, "dp", 1)
        first = lax.axis_index("dp") == 0
        own = jnp.concatenate([jnp.where(first, own, other), jnp.where(first, other, own)], axis=1)
    else:
        own = lax.all_gather(own, "dp", axis=1, tiled=True)
    return lax.all_gather(own, "fsdp", axis=0, tiled=True)


def sum_terms(terms):
    total = terms[0].astype(jnp.float32)
    for term in terms[1:]:
        total = total + term.astype(jnp.float32)
    return total


def scatter_rows(partial, order):
    fsdp_bits = bits_of(lax.axis_size("fsdp"))
    dp_bits = bits_of(lax.axis_size("dp"))
    block = partial.shape[0] >> fsdp_bits
    width = partial.shape[1]
    place = {"fsdp": lax.axis_index("fsdp"), "dp": lax.axis_index("dp")}
    terms = [
        (
            partial.reshape((2,) * fsdp_bits + (block, width)),
            list(range(fsdp_bits - 1, -1, -1)),
            list(range(dp_bits - 1, -1, -1)),
        )
    ]
    left = {
        "fsdp": list(range(fsdp_bits - 1, -1, -1)),
        "dp": list(range(dp_bits - 1, -1, -1)),
    }

    def part_of(term, flipped):
        array, own_bits, own_dp = term
        starts, sizes = [], []
        for bit in own_bits:
            if bit in left["fsdp"] and ("fsdp", bit) != flipped:
                starts.append(0)
                sizes.append(2)
            else:
                value = (place["fsdp"] >> bit) & 1
                starts.append(1 - value if ("fsdp", bit) == flipped else value)
                sizes.append(1)
        span = array.shape[-1]
        offset = 0
        for bit in own_dp:
            if bit not in left["dp"] or ("dp", bit) == flipped:
                span //= 2
                value = (place["dp"] >> bit) & 1
                offset = offset + span * (1 - value if ("dp", bit) == flipped else value)
        starts += [0, offset]
        sizes += [block, span]
        taken = lax.dynamic_slice(array, starts, sizes)
        kept = [bit for bit in left["fsdp"] if ("fsdp", bit) != flipped]
        return taken.reshape((2,) * len(kept) + (block, span))

    for axis_name, bit in order:
        sent = sum_terms([part_of(term, (axis_name, bit)) for term in terms]).astype(jnp.bfloat16)
        received = swap(sent, axis_name, 1 << bit)
        left[axis_name].remove(bit)
        terms.append((received, list(left["fsdp"]), list(left["dp"])))
    return sum_terms([part_of(term, None) for term in terms]).T


def all_sum(value):
    for axis_name in ("fsdp", "dp"):
        for bit in range(bits_of(lax.axis_size(axis_name))):
            value = value + swap(value, axis_name, 1 << bit)
    return value


def exchange_orders():
    fsdp_bits = bits_of(lax.axis_size("fsdp"))
    dp_steps = [("dp", bit) for bit in range(bits_of(lax.axis_size("dp")) - 1, -1, -1)]
    first = [("fsdp", 0)]
    second = [("fsdp", 1)]
    rest = [("fsdp", bit) for bit in range(2, fsdp_bits)]
    return (first + second + dp_steps + rest, first + dp_steps + second + rest)


def masked_scores(queries, key_heads, segment, score_scale):
    seq_rows = segment.shape[1]
    scores = (
        jnp.einsum("gqhd,gkhd->ghqk", queries, key_heads, preferred_element_type=jnp.float32)
        * score_scale
    )
    places = lax.broadcasted_iota(jnp.int32, (seq_rows, seq_rows), 0)
    columns = lax.broadcasted_iota(jnp.int32, (seq_rows, seq_rows), 1)
    allowed = (columns <= places)[None] & (segment[:, :, None] == segment[:, None, :])
    return jnp.where(allowed[:, None], scores, neg_big)


def dot_of(left, right, left_dim, right_dim):
    return lax.dot_general(
        left, right, (((left_dim,), (right_dim,)), ((), ())), preferred_element_type=jnp.float32
    )


def allowed_block(rows_first, columns_first, row_segments, column_segments):
    shape = (row_segments.shape[0], column_segments.shape[1])
    places = rows_first + lax.broadcasted_iota(jnp.int32, shape, 0)
    columns = columns_first + lax.broadcasted_iota(jnp.int32, shape, 1)
    return (columns <= places) & (row_segments == column_segments)


def attention_forward_kernel(row_seg_ref, col_seg_ref, q_ref, k_ref, v_ref, o_ref, log_ref, *, block):
    seq_rows = q_ref.shape[0]
    heads_here = q_ref.shape[1] // HD
    score_scale = 1.0 / math.sqrt(HD)
    for first in range(0, seq_rows, block):
        last = first + block
        allowed = allowed_block(first, 0, row_seg_ref[first:last, :], col_seg_ref[0, :, :last])
        outs, logs = [], []
        for head in range(heads_here):
            lanes = slice(head * HD, (head + 1) * HD)
            scores = dot_of(q_ref[first:last, lanes], k_ref[:last, lanes], 1, 1) * score_scale
            scores = jnp.where(allowed, scores, neg_big)
            peak = jnp.max(scores, axis=-1, keepdims=True)
            powers = jnp.exp(scores - peak)
            total = jnp.sum(powers, axis=-1, keepdims=True)
            probs = (powers * (1.0 / total)).astype(jnp.bfloat16)
            outs.append(dot_of(probs, v_ref[:last, lanes], 1, 0))
            logs.append(peak + jnp.log(total))
        o_ref[first:last, :] = jnp.concatenate(outs, axis=1).astype(jnp.bfloat16)
        log_ref[0, first:last, :] = jnp.concatenate(logs, axis=1)


def attention_backward_kernel(
    row_seg_ref, col_seg_ref, q_ref, k_ref, v_ref, g_ref, log_ref, out_ref, *, block
):
    seq_rows = q_ref.shape[0]
    heads_here = q_ref.shape[1] // HD
    score_scale = 1.0 / math.sqrt(HD)
    dk_sums = [[None] * (seq_rows // block) for _ in range(heads_here)]
    dv_sums = [[None] * (seq_rows // block) for _ in range(heads_here)]
    for first in range(0, seq_rows, block):
        last = first + block
        allowed = allowed_block(first, 0, row_seg_ref[first:last, :], col_seg_ref[0, :, :last])
        dqs = []
        for head in range(heads_here):
            lanes = slice(head * HD, (head + 1) * HD)
            queries = q_ref[first:last, lanes]
            key_part = k_ref[:last, lanes]
            upstream = g_ref[first:last, lanes]
            scores = dot_of(queries, key_part, 1, 1) * score_scale
            scores = jnp.where(allowed, scores, neg_big)
            probs = jnp.exp(scores - log_ref[0, first:last, head : head + 1])
            grad_probs = dot_of(upstream, v_ref[:last, lanes], 1, 1)
            inner = jnp.sum(probs * grad_probs, axis=-1, keepdims=True)
            grad_scores = (probs * (grad_probs - inner)).astype(jnp.bfloat16)
            probs_b = probs.astype(jnp.bfloat16)
            dqs.append(dot_of(grad_scores, key_part, 1, 0) * score_scale)
            dv_part = dot_of(probs_b, upstream, 0, 0)
            dk_part = dot_of(grad_scores, queries, 0, 0)
            for index in range(last // block):
                span = slice(index * block, (index + 1) * block)
                old_v, old_k = dv_sums[head][index], dk_sums[head][index]
                dv_sums[head][index] = dv_part[span] if old_v is None else old_v + dv_part[span]
                dk_sums[head][index] = dk_part[span] if old_k is None else old_k + dk_part[span]
        out_ref[0, first:last, :] = jnp.concatenate(dqs, axis=1).astype(jnp.bfloat16)
    for index in range(seq_rows // block):
        span = slice(index * block, (index + 1) * block)
        out_ref[1, span, :] = (
            jnp.concatenate([dk_sums[head][index] for head in range(heads_here)], axis=1)
            * score_scale
        ).astype(jnp.bfloat16)
        out_ref[2, span, :] = jnp.concatenate(
            [dv_sums[head][index] for head in range(heads_here)], axis=1
        ).astype(jnp.bfloat16)


PAIR = 2


def attention_call(kernel, operands, segments, output, log_operand, table, filled=None):
    groups, seq_rows = segments.shape
    lanes = PAIR * HD
    rows = groups * seq_rows
    seq_block = pl.BlockSpec((seq_rows, lanes), lambda group, pair, table: (group, table[pair]))
    log_block = pl.BlockSpec((1, seq_rows, PAIR), lambda group, pair, table: (table[pair], group, 0))
    three_block = pl.BlockSpec(
        (3, seq_rows, lanes), lambda group, pair, table: (0, group, table[pair])
    )
    specs = {
        "seq": (seq_block, jax.ShapeDtypeStruct((rows, HEADS * HD), jnp.bfloat16)),
        "log": (log_block, jax.ShapeDtypeStruct((HEADS // PAIR, rows, PAIR), jnp.float32)),
        "three": (three_block, jax.ShapeDtypeStruct((3, rows, HEADS * HD), jnp.bfloat16)),
    }
    inputs = [segments.reshape(rows, 1), segments.reshape(groups, 1, seq_rows), *operands]
    in_specs = [
        pl.BlockSpec((seq_rows, 1), lambda group, pair, table: (group, 0)),
        pl.BlockSpec((1, 1, seq_rows), lambda group, pair, table: (group, 0, 0)),
    ] + [seq_block] * len(operands)
    if log_operand is not None:
        inputs.append(log_operand)
        in_specs.append(log_block)
    aliases = {}
    body = functools.partial(kernel, block=min(256, seq_rows))

    def inner(table_ref, *refs):
        count = len(in_specs)
        body(*refs[: count - (filled is not None)], *refs[count:])

    if filled is not None:
        aliases = {len(inputs) + 1: 0}
        inputs.append(filled)
        in_specs.append(pl.BlockSpec(memory_space=pl.ANY))
    return pl.pallas_call(
        inner,
        grid_spec=pltpu.PrefetchScalarGridSpec(
            num_scalar_prefetch=1,
            grid=(groups, table.shape[0]),
            in_specs=in_specs,
            out_specs=[specs[kind][0] for kind in output],
        ),
        out_shape=[specs[kind][1] for kind in output],
        input_output_aliases=aliases,
        name=kernel.__name__,
    )(table, *inputs)


def attention_forward(queries, key_heads, value_heads, segments, table=None):
    if table is None:
        table = jnp.arange(HEADS // PAIR, dtype=jnp.int32)
    return attention_call(
        attention_forward_kernel,
        (queries, key_heads, value_heads),
        segments,
        ("seq", "log"),
        None,
        table,
    )


def attention_backward(
    queries, key_heads, value_heads, log_total, segments, grad_mixed, table=None, filled=None
):
    if table is None:
        table = jnp.arange(HEADS // PAIR, dtype=jnp.int32)
    return attention_call(
        attention_backward_kernel,
        (queries, key_heads, value_heads, grad_mixed),
        segments,
        ("three",),
        log_total,
        table,
        filled,
    )[0]


def tie(value, *earlier):
    return lax.optimization_barrier((value, *earlier))[0] if earlier else value


def all_sum_paired(value):
    for rounds in ([("fsdp", 1), ("fsdp", 2), ("fsdp", 3)], [("fsdp", 4), ("fsdp", 8), ("fsdp", 12)], [("dp", 1)]):
        value = sum_terms([value] + [swap(value, axis_name, mask) for axis_name, mask in rounds])
    return value


class Fetch:
    def __init__(self, shards, places, y_first, *earlier):
        own = [shard.T for shard in shards]
        self.heights = [part.shape[0] for part in own]
        self.places, self.y_first = places, y_first
        own = own[0] if len(own) == 1 else jnp.concatenate(own, axis=0)
        self.own = tie(own, *earlier)[None]
        self.steps = [("dp", 1), ("fsdp", 2)]
        if y_first:
            self.steps = self.steps[::-1]

    def first(self):
        for mask in (8, 4):
            self.own = jnp.concatenate([self.own, swap(self.own, "fsdp", mask)], axis=0)
        return self.own

    def second(self, *earlier):
        own = tie(self.own, *earlier)
        self.own = jnp.stack([own, swap(own, *self.steps[0])])
        return self.own

    def third(self, *earlier):
        own = tie(self.own, *earlier)
        pieces = [own, swap(own, *self.steps[1])]
        pieces += [swap(piece, "fsdp", 1) for piece in pieces]
        self.pieces = pieces
        return pieces[1]

    def whole(self):
        return assemble(self.pieces, self.heights, self.places, self.y_first)


def assemble_kernel(place_ref, *refs, heights, y_first):
    piece_refs, out_refs = refs[:4], refs[4:]
    half = piece_refs[0].shape[-1]
    own_y, own_core, own_x = place_ref[4], place_ref[5], place_ref[6]
    for index, piece_ref in enumerate(piece_refs):
        second, core = index % 2, own_core ^ (index // 2)
        for first in range(2):
            y, x = (first, second) if y_first else (second, first)
            lanes = pl.ds(pl.multiple_of((own_x ^ x) * half, half), half)
            start = 0
            for height, out_ref in zip(heights, out_refs):
                out_ref[0, own_y ^ y, core, :, lanes] = piece_ref[first, 0, start : start + height, :]
                start += height


def assemble(pieces, heights, places, y_first):
    _, zs, height, half = pieces[0].shape
    outs = pl.pallas_call(
        functools.partial(assemble_kernel, heights=heights, y_first=y_first),
        grid_spec=pltpu.PrefetchScalarGridSpec(
            num_scalar_prefetch=1,
            grid=(zs,),
            in_specs=[pl.BlockSpec((2, 1, height, half), lambda i, place: (0, i, 0, 0))] * 4,
            out_specs=[
                pl.BlockSpec((1, 2, 2, part, 2 * half), lambda i, place: (place[i], 0, 0, 0, 0))
                for part in heights
            ],
        ),
        out_shape=[
            jax.ShapeDtypeStruct((zs, 2, 2, part, 2 * half), jnp.bfloat16) for part in heights
        ],
        name="assemble",
    )(places, *pieces)
    return [out.reshape(-1, 2 * half) for out in outs]


def relative_places():
    at = lax.axis_index("fsdp")
    z, y, core = at >> 2, (at >> 1) & 1, at & 1
    zs = [z ^ (j >> 1) ^ ((j & 1) << 1) for j in range(4)]
    return jnp.stack([*zs, y, core, lax.axis_index("dp")]).astype(jnp.int32)


def grad_kernel(table_ref, halves_ref, d0_ref, d1_ref, act0_ref, act1_ref, out_ref):
    half = act0_ref.shape[1]
    turned = jnp.concatenate([d0_ref[...], d1_ref[...]], axis=1).T
    shape = out_ref.shape[:2] + (half,)
    for index, act_ref in enumerate((act0_ref, act1_ref)):
        sums = jnp.dot(turned, act_ref[...], preferred_element_type=jnp.float32)
        out_ref[:, :, index * half : (index + 1) * half] = sums.astype(jnp.bfloat16).reshape(shape)


def grad_blocks(upstream, acts, blocks, halves):
    rows, width = acts.shape
    height = upstream.shape[1] // lax.axis_size("fsdp")
    count = blocks.shape[0]
    return pl.pallas_call(
        grad_kernel,
        grid_spec=pltpu.PrefetchScalarGridSpec(
            num_scalar_prefetch=2,
            grid=(count // 2,),
            in_specs=[
                pl.BlockSpec((rows, height), lambda i, table, at: (0, table[2 * i])),
                pl.BlockSpec((rows, height), lambda i, table, at: (0, table[2 * i + 1])),
                pl.BlockSpec((rows, width // 2), lambda i, table, at: (0, at[0])),
                pl.BlockSpec((rows, width // 2), lambda i, table, at: (0, at[1])),
            ],
            out_specs=pl.BlockSpec((2, height, width), lambda i, table, at: (i, 0, 0)),
        ),
        out_shape=jax.ShapeDtypeStruct((count, height, width), jnp.bfloat16),
        name="weight_grad",
    )(blocks, halves, upstream, upstream, acts, acts)


FOUR = 4


def grad_pair_kernel(table_ref, acts_at_ref, core_ref, *refs):
    d_refs, (act_ref, sent_ref, kept_ref, sums_ref) = refs[:FOUR], refs[FOUR:]
    turned = jnp.concatenate([ref[0] for ref in d_refs], axis=1).T
    sums_ref[...] = jnp.dot(turned, act_ref[...], preferred_element_type=jnp.float32)
    height = kept_ref.shape[-2]
    core = core_ref[0]
    for index in range(FOUR):
        base = index * 2 * height
        kept_at = pl.multiple_of(base + core * height, height)
        sent_at = pl.multiple_of(base + (1 - core) * height, height)
        kept_ref[index, 0] = sums_ref[pl.ds(kept_at, height), :].astype(jnp.bfloat16)
        sent_ref[index, 0] = sums_ref[pl.ds(sent_at, height), :].astype(jnp.bfloat16)


def grad_pairs(upstream, acts, pairs, act_blocks, core):
    rows, width = acts.shape
    many = upstream.shape[0]
    height = upstream.shape[2] // lax.axis_size("fsdp")
    part = width // act_blocks.shape[0]
    count = pairs.shape[0]
    shape = jax.ShapeDtypeStruct((count, many, height, width), jnp.bfloat16)
    out_block = pl.BlockSpec((FOUR, 1, height, part), lambda k, m, i, *tables: (i, m, 0, k))

    def pair_block(place):
        return pl.BlockSpec(
            (1, rows, 2 * height), lambda k, m, i, table, *_: (m, 0, table[FOUR * i + place])
        )

    return pl.pallas_call(
        grad_pair_kernel,
        grid_spec=pltpu.PrefetchScalarGridSpec(
            num_scalar_prefetch=3,
            grid=(act_blocks.shape[0], many, count // FOUR),
            in_specs=[pair_block(place) for place in range(FOUR)]
            + [pl.BlockSpec((rows, part), lambda k, m, i, table, acts_at, _: (0, acts_at[k]))],
            out_specs=[out_block, out_block],
            scratch_shapes=[pltpu.VMEM((FOUR * 2 * height, part), jnp.float32)],
        ),
        out_shape=[shape, shape],
        name="weight_grad_pairs",
    )(pairs, act_blocks, core, *([upstream] * FOUR), acts)


def step(exchange, *earlier):
    return exchange.send(earlier)


def primed(generator):
    def begin(*arguments):
        exchange = generator(*arguments)
        next(exchange)
        return exchange

    return begin


def held(terms, earlier):
    return terms[:-1] + [tie(terms[-1], *earlier)]


@primed
def scatter_pairs(sent, kept, y_first):
    half = kept.shape[-1] // 2
    yield
    terms = [kept, swap(sent, "fsdp", 1)]
    earlier = yield sent
    for axis_name in ("fsdp", "dp") if y_first else ("dp", "fsdp"):
        terms = held(terms, earlier)
        if axis_name == "fsdp":
            given = sum_terms([term[4:] for term in terms]).astype(jnp.bfloat16)
            terms = [term[:4] for term in terms] + [swap(given, "fsdp", 2)]
        else:
            given = sum_terms([term[..., half:] for term in terms]).astype(jnp.bfloat16)
            terms = [term[..., :half] for term in terms] + [swap(given, "dp", 1)]
        earlier = yield given
    yield from scatter_last(terms, earlier)


def scatter_last(terms, earlier):
    for mask, at in ((4, 2), (8, 1)):
        terms = held(terms, earlier)
        given = sum_terms([term[at : 2 * at] for term in terms]).astype(jnp.bfloat16)
        terms = [term[:at] for term in terms] + [swap(given, "fsdp", mask)]
        earlier = yield given
    yield sum_terms([term[0] for term in held(terms, earlier)])


@primed
def scatter_split(far, near):
    yield
    far_sent, far_kept = far()
    terms = [far_kept, swap(far_sent, "fsdp", 1)]
    earlier = yield far_sent
    given = sum_terms(held(terms, earlier)).astype(jnp.bfloat16)
    got = swap(given, "fsdp", 2)
    yield given
    sent, kept = near()
    half = kept.shape[-1] // 2
    terms = [kept, got, swap(sent, "fsdp", 1)]
    earlier = yield sent
    terms = held(terms, earlier)
    given = sum_terms([term[..., half:] for term in terms]).astype(jnp.bfloat16)
    terms = [term[..., :half] for term in terms] + [swap(given, "dp", 1)]
    earlier = yield given
    yield from scatter_last(terms, earlier)


def grad_tables(places):
    z, y, core, x = places[:4], places[4], places[5], places[6:7]
    pairs = jnp.concatenate([z * 2 + y, z * 2 + (1 - y)])
    halves = jnp.concatenate([x, 1 - x])
    quarters = jnp.concatenate([2 * x, 2 * x + 1, 2 - 2 * x, 3 - 2 * x])
    return pairs, pairs * 2 + (1 - core), pairs * 2 + core, halves, quarters, places[5:6]


def per_device_paired(
    rows, segments, norm_gains, w_query, w_key, w_value, w_output, w_gate, w_up, w_down, cotangent
):
    gain_attn = norm_gains[0]
    gain_mlp = norm_gains[1]
    places = relative_places()
    pairs, sent_blocks, kept_blocks, halves, quarters, core = grad_tables(places)

    source = rows.astype(jnp.float32)
    normed, inverse_attn = norm_forward(source, gain_attn)
    normed_b = normed.astype(jnp.bfloat16)

    middle = w_down.shape[1] // 2
    fetch_a = Fetch((w_query, w_key), places, False)
    fetch_b = Fetch((w_value, w_output), places, True)
    begun = (fetch_a.first(), fetch_b.first())
    fetch_gate = Fetch((w_gate,), places, False, *begun)
    fetch_up = Fetch((w_up,), places, True, *begun)
    begun = (fetch_a.second(), fetch_b.second())
    begun_mlp = (fetch_gate.first(), fetch_up.first())
    begun = (fetch_a.third(), fetch_b.third())
    fetch_c = Fetch((w_down,), places, False, *begun_mlp)
    begun_mlp = (fetch_gate.second(*begun), fetch_up.second(*begun))
    begun_down = fetch_c.first()
    full_query, full_key = fetch_a.whole()
    full_value, full_output = fetch_b.whole()
    queries = product_right(normed_b, full_query).astype(jnp.bfloat16)
    key_heads = product_right(normed_b, full_key).astype(jnp.bfloat16)
    value_heads = product_right(normed_b, full_value).astype(jnp.bfloat16)
    queries = tie(queries, *begun_mlp, begun_down)
    begun_mlp = (fetch_gate.third(), fetch_up.third())
    mixed_heads, log_total = attention_forward(queries, key_heads, value_heads, segments)
    begun_down = fetch_c.second(mixed_heads)
    hidden = source + product_right(mixed_heads, full_output)
    normed_two, inverse_mlp = norm_forward(hidden, gain_mlp)
    normed_two_b = normed_two.astype(jnp.bfloat16)
    (full_gate,) = fetch_gate.whole()
    gate_value = product_right(normed_two_b, full_gate)
    fetch_c.third(gate_value)
    (full_up,) = fetch_up.whole()
    up_value = product_right(normed_two_b, full_up)
    sigmoid_gate = jax.nn.sigmoid(gate_value)
    activated = gate_value * sigmoid_gate
    inner_rows = (activated * up_value).astype(jnp.bfloat16)

    grad_out = cotangent.astype(jnp.float32)
    down = scatter_pairs(*grad_pairs(cotangent[None], inner_rows, pairs, quarters, core), True)
    (full_down,) = fetch_c.whole()
    result = hidden + product_right(tie(inner_rows, step(down)), full_down)
    layer_out = result.astype(jnp.bfloat16)
    grad_inner = product(tie(cotangent, layer_out, step(down, layer_out)), full_down)
    grad_up = (grad_inner * activated).astype(jnp.bfloat16)
    grad_gate = (
        grad_inner * up_value * sigmoid_gate * (1.0 + gate_value * (1.0 - sigmoid_gate))
    ).astype(jnp.bfloat16)
    gate_sent = grad_blocks(grad_gate, normed_two_b, sent_blocks, halves)
    gate_kept = grad_blocks(tie(grad_gate, gate_sent), normed_two_b, kept_blocks, halves)
    gate = scatter_pairs(gate_sent, gate_kept, False)
    step(gate)
    grad_up = tie(grad_up, gate_kept)
    up_sent = grad_blocks(grad_up, normed_two_b, sent_blocks, halves)
    grad_up_kept = tie(grad_up, up_sent, step(gate, up_sent))
    up_kept = grad_blocks(grad_up_kept, normed_two_b, kept_blocks, halves)
    up = scatter_pairs(up_sent, up_kept, True)
    step(up)
    part = product(tie(grad_gate, up_kept), full_gate)
    grad_up = tie(grad_up, part, step(up, part))
    grad_normed_two = part + product(grad_up, full_up)
    grad_normed_two = tie(grad_normed_two, step(down, grad_normed_two))
    back_mlp, gain_mlp_term = norm_backward(hidden, inverse_mlp, gain_mlp, grad_normed_two)
    grad_hidden = grad_out + back_mlp
    grad_hidden_b = grad_hidden.astype(jnp.bfloat16)
    output = scatter_pairs(
        *grad_pairs(grad_hidden_b[None], mixed_heads, pairs, halves, core), False
    )
    grad_mixed = product(tie(grad_hidden_b, step(output)), full_output).astype(jnp.bfloat16)
    grad_mixed = tie(grad_mixed, step(gate, grad_mixed), step(output, grad_mixed))
    begun = []

    def far():
        begun.append(
            attention_backward(
                queries, key_heads, value_heads, log_total, segments, grad_mixed, pairs[4:]
            )
        )
        return grad_pairs(begun[0], normed_b, pairs[4:], halves, core)

    def near():
        begun.append(
            attention_backward(
                queries,
                key_heads,
                value_heads,
                log_total,
                segments,
                tie(grad_mixed, *waits),
                pairs[:4],
                begun[0],
            )
        )
        return grad_pairs(begun[1], normed_b, pairs[:4], halves, core)

    attn = scatter_split(far, near)
    sent = step(attn)
    waits = [step(attn, sent), step(down, sent), step(up, sent)]
    sent = step(attn)
    grad_attn = tie(begun[1], sent, *(step(one, sent) for one in (gate, down, output)))
    grad_normed = product(grad_attn[0], full_query) + product(grad_attn[1], full_key)
    grad_attn = tie(grad_attn, grad_normed, step(attn, grad_normed))
    grad_normed = grad_normed + product(grad_attn[2], full_value)
    grad_normed = tie(grad_normed, *(step(one, grad_normed) for one in (up, gate, output)))
    back_attn, gain_attn_term = norm_backward(source, inverse_attn, gain_attn, grad_normed)
    rows_grad = grad_hidden + back_attn
    gains_grad = all_sum_paired(jnp.stack([gain_attn_term, gain_mlp_term]))
    for one in (attn, up, output):
        step(one, grad_normed)
    step(attn, rows_grad)
    up_sum, gate_sum, output_sum, down_sum, attn_sum = (
        step(one, rows_grad) for one in (up, gate, output, down, attn)
    )
    return (
        layer_out,
        rows_grad,
        gains_grad,
        attn_sum[0].T,
        attn_sum[1].T,
        attn_sum[2].T,
        output_sum[0].T,
        gate_sum.T,
        up_sum.T,
        down_sum[0].T,
    )


def per_device_any(
    rows, segments, norm_gains, w_query, w_key, w_value, w_output, w_gate, w_up, w_down, cotangent
):
    gain_attn = norm_gains[0]
    gain_mlp = norm_gains[1]
    order_a, order_b = exchange_orders()
    full_query = fetch_rows(w_query)
    full_key = fetch_rows(w_key)
    full_value = fetch_rows(w_value)
    full_output = fetch_rows(w_output)
    full_gate = fetch_rows(w_gate)
    full_up = fetch_rows(w_up)
    full_down = fetch_rows(w_down)

    source = rows.astype(jnp.float32)
    normed, inverse_attn = norm_forward(source, gain_attn)
    normed_b = normed.astype(jnp.bfloat16)
    queries = product_right(normed_b, full_query).astype(jnp.bfloat16)
    key_heads = product_right(normed_b, full_key).astype(jnp.bfloat16)
    value_heads = product_right(normed_b, full_value).astype(jnp.bfloat16)
    mixed_heads, log_total = attention_forward(
        queries, key_heads, value_heads, segments
    )
    hidden = source + product_right(mixed_heads, full_output)
    normed_two, inverse_mlp = norm_forward(hidden, gain_mlp)
    normed_two_b = normed_two.astype(jnp.bfloat16)
    gate_value = product_right(normed_two_b, full_gate)
    up_value = product_right(normed_two_b, full_up)
    sigmoid_gate = jax.nn.sigmoid(gate_value)
    activated = gate_value * sigmoid_gate
    inner_rows = (activated * up_value).astype(jnp.bfloat16)
    result = hidden + product_right(inner_rows, full_down)
    layer_out = result.astype(jnp.bfloat16)

    grad_out = cotangent.astype(jnp.float32)
    down_grad = scatter_rows(
        product_left(cotangent, inner_rows).astype(jnp.bfloat16), order_a
    )
    grad_inner = product(cotangent, full_down)
    grad_up = (grad_inner * activated).astype(jnp.bfloat16)
    grad_gate = (
        grad_inner * up_value * sigmoid_gate * (1.0 + gate_value * (1.0 - sigmoid_gate))
    ).astype(jnp.bfloat16)
    gate_grad = scatter_rows(
        product_left(grad_gate, normed_two_b).astype(jnp.bfloat16), order_b
    )
    up_grad = scatter_rows(product_left(grad_up, normed_two_b).astype(jnp.bfloat16), order_a)
    grad_normed_two = product(grad_gate, full_gate) + product(grad_up, full_up)
    back_mlp, gain_mlp_term = norm_backward(hidden, inverse_mlp, gain_mlp, grad_normed_two)
    grad_hidden = grad_out + back_mlp
    grad_hidden_b = grad_hidden.astype(jnp.bfloat16)
    output_grad = scatter_rows(
        product_left(grad_hidden_b, mixed_heads).astype(jnp.bfloat16), order_b
    )
    grad_mixed = product(grad_hidden_b, full_output).astype(jnp.bfloat16)
    grad_queries, grad_keys, grad_values = attention_backward(
        queries, key_heads, value_heads, log_total, segments, grad_mixed
    )
    query_grad = scatter_rows(product_left(grad_queries, normed_b).astype(jnp.bfloat16), order_a)
    key_grad = scatter_rows(product_left(grad_keys, normed_b).astype(jnp.bfloat16), order_b)
    value_grad = scatter_rows(product_left(grad_values, normed_b).astype(jnp.bfloat16), order_a)
    grad_normed = (
        product(grad_queries, full_query)
        + product(grad_keys, full_key)
        + product(grad_values, full_value)
    )
    back_attn, gain_attn_term = norm_backward(source, inverse_attn, gain_attn, grad_normed)
    rows_grad = grad_hidden + back_attn
    gains_grad = all_sum(jnp.stack([gain_attn_term, gain_mlp_term]))
    return (
        layer_out,
        rows_grad,
        gains_grad,
        query_grad,
        key_grad,
        value_grad,
        output_grad,
        gate_grad,
        up_grad,
        down_grad,
    )


def solution(mesh):
    split_rows = P(("dp", "fsdp"), None)
    split_weight = P("dp", "fsdp")
    paired = mesh.shape["dp"] == 2 and mesh.shape["fsdp"] == 16
    return jax.shard_map(
        per_device_paired if paired else per_device_any,
        mesh=mesh,
        in_specs=(split_rows, split_rows, P()) + (split_weight,) * 7 + (split_rows,),
        out_specs=(split_rows, split_rows, P()) + (split_weight,) * 7,
        check_vma=False,
    )
```
